256 devices in a mesh: pole: 16 (over x, y_hi, core), blk: 16 (over y_lo, z).
Axes of the slice: x: 4, y: 4 (y_hi: 2, y_lo: 2; y = y_hi * 2 + y_lo), z: 8, core: 2. Of those that a mesh axis runs over, the one named last changes fastest.
Arguments:
- inverse: float32 [16, 4096, 8192], P('pole', None, 'blk'), may hold values from -6 to 6
- factor: float32 [16, 3, 1280, 512], P('pole', None, 'blk'), may hold values from -0.125 to 0.125
- diag_inverse: float32 [16, 3, 256, 512], P('pole'), may hold values from -6 to 6
- residues: float32 [16, 2], P('pole'), may hold values from -0.6 to 0.6
- row_lists: int32 [3, 5], replicated, may hold values from 0 to 15, as said below
- block_slot: int32 [16], replicated, may hold values from 0 to 15, each once
Outputs:
- density_rows: float32 [3, 256, 4096], P(None, 'pole', 'blk')
- density_diag: float32 [3, 256, 256], P(None, 'pole')
The draws below stay inside these ranges and needn't reach their ends.
Inputs may be any that keep to these rules, and one draw needn't show every extreme that they name: `row_lists`: each row names 5 different ancestor blocks in ascending order, and every row names block 15. `block_slot`: each slot is named once.
All inputs are finite; a program needn't handle non-finite values.
Results may differ from the reference program's by a relative error of at most 0.0001.
Values sent between devices are 32-bit elements; how exact they have to be, the bound alone decides.
No kernel may reach another device: no remote copies, remote signals or barrier semaphores. Data moves between devices by JAX's collectives and lax.ppermute only.
A program may use at most 128 MiB of HBM per device.

```python
import jax
import jax.numpy as jnp
from jax import lax

W = 256
M = 5
NB = 16
NS = 3
POLES = 16


def draw_row_lists(key, part):
    subkeys = jax.random.split(jax.random.fold_in(key, 17), NS)

    def single(subkey):
        order = jax.random.permutation(subkey, NB - 1).astype(jnp.int32)
        picked = order[:M - 1]
        root_block = jnp.full((1,), NB - 1, jnp.int32)
        return jnp.sort(jnp.concatenate([picked, root_block])).astype(jnp.int32)
    return jax.vmap(single)(subkeys)


def block_levels(stream_key, extent, cuts, smallest, largest):
    loudness = 1.0
    for position, blocks in cuts:
        heights = jax.random.uniform(jax.random.fold_in(jax.random.fold_in(stream_key, 6), position), (blocks,), jnp.float32, smallest / len(cuts), largest / len(cuts))
        loudness = loudness * jnp.repeat(jnp.exp(heights), extent[position] // blocks).reshape((-1,) + (1,) * (len(extent) - 1 - position))
    return loudness


def gaussian(key, shape, scale, bound, cuts=(), kind=jnp.bfloat16):
    result = jax.random.normal(key, shape, jnp.float32) * scale
    if len(cuts) > 0:
        result = block_levels(key, shape, cuts, -0.22, 0.18) * result
    return jnp.clip(result, min=-bound, max=bound).astype(kind)


def setup_inputs(seed: int = 0) -> dict:
    splits = jax.random.split(jax.random.key(seed), 7)
    return {
        "inverse": gaussian(splits[0], (POLES, NB * W, NB * 2 * W), 1.0, 6.0, ((0, 16), (2, 16)), jnp.float32),
        "factor": gaussian(splits[1], (POLES, NS, M * W, 2 * W), (2 * M * W) ** -0.5, 0.125, ((0, 16), (2, 16)), jnp.float32),
        "diag_inverse": gaussian(splits[2], (POLES, NS, W, 2 * W), 1.0, 6.0, ((0, 16),), jnp.float32),
        "residues": jnp.clip(jax.random.uniform(splits[3], (POLES, 2), jnp.float32, -0.6, 0.6) * block_levels(splits[3], (POLES, 2), ((0, 16),), -0.4, 0.0), -0.6, 0.6),
        "row_lists": draw_row_lists(jax.random.fold_in(splits[6], 71), 0),
        "block_slot": jax.random.permutation(splits[5], NB).astype(jnp.int32),
    }


HIGH = lax.Precision.HIGHEST


def complex_stack(tile, width):
    real = tile[:, :width]
    imag = tile[:, width:]
    upper = jnp.concatenate([real, imag], 1)
    lower = jnp.concatenate([-imag, real], 1)
    return jnp.concatenate([upper, lower], 0)


def pole_terms(inverse_pole, factor_pole, diag_pole, weights, row_lists, block_slot):
    blocks = inverse_pole.reshape(NB, W, NB, 2 * W)
    rows_list = []
    diag_list = []
    for node in range(NS):
        slots = jnp.take(block_slot, row_lists[node], axis=0).astype(jnp.int32)
        chosen = jnp.take(jnp.take(blocks, slots, axis=0), slots, axis=2)
        matrix = chosen.reshape(M * W, M * 2 * W)
        tiles = factor_pole[node].reshape(M, W, 2 * W)
        stacked = jnp.concatenate([complex_stack(tiles[m], W) for m in range(M)], 0)
        product = jnp.dot(matrix, stacked, precision=HIGH, preferred_element_type=jnp.float32)
        column = -product
        crossed = jnp.dot(factor_pole[node].T, column, precision=HIGH, preferred_element_type=jnp.float32)
        real = diag_pole[node, :, :W] - (crossed[:W, :W] - crossed[W:, W:])
        imag = diag_pole[node, :, W:] - (crossed[:W, W:] + crossed[W:, :W])
        diag_list.append(weights[0] * imag + weights[1] * real)
        pieces = column.reshape(M, W, 2 * W)
        term = weights[0] * pieces[:, :, W:] + weights[1] * pieces[:, :, :W]
        placed = jnp.zeros((NB, W, W), jnp.float32).at[slots].set(term)
        rows_list.append(jnp.transpose(placed, (2, 0, 1)).reshape(W, NB * W))
    return jnp.stack(rows_list), jnp.stack(diag_list)


def reference(inverse, factor, diag_inverse, residues, row_lists, block_slot):
    def accumulate(carry, pole):
        inverse_pole, factor_pole, diag_pole, weights = pole
        rows_term, diag_term = pole_terms(inverse_pole, factor_pole, diag_pole, weights, row_lists, block_slot)
        return (carry[0] + rows_term, carry[1] + diag_term), None

    start = (jnp.zeros((NS, W, NB * W), jnp.float32), jnp.zeros((NS, W, W), jnp.float32))
    totals, unused = lax.scan(accumulate, start, (inverse, factor, diag_inverse, residues))
    return totals[0], totals[1]
```

```python
import functools

import jax
import jax.numpy as jnp
from jax import lax
from jax.experimental import pallas as pl
from jax.experimental.pallas import tpu as pltpu
from jax.sharding import PartitionSpec as P


NX, NH, NC = 4, 2, 2
NY, NZ = 2, 8


def pole_perm(move):
    out = []
    for x in range(NX):
        for h in range(NH):
            for c in range(NC):
                a, b, d = move(x, h, c)
                out.append(((x * NH + h) * NC + c, (a * NH + b) * NC + d))
    return out


def blk_perm(move):
    out = []
    for y in range(NY):
        for z in range(NZ):
            a, b = move(y, z)
            out.append((y * NZ + z, a * NZ + b))
    return out


def shift_z(step):
    return blk_perm(lambda y, z: (y, (z + step) % NZ))


def shift_x(step):
    return pole_perm(lambda x, h, c: ((x + step) % NX, h, c))


FLIP_Y = blk_perm(lambda y, z: (1 - y, z))
FLIP_H = pole_perm(lambda x, h, c: (x, 1 - h, c))
FLIP_C = pole_perm(lambda x, h, c: (x, h, 1 - c))


def split(value):
    high = value.astype(jnp.bfloat16)
    low = (value - high.astype(jnp.float32)).astype(jnp.bfloat16)
    return high, low


def dot3(left, right, contract):
    dims = (contract, ((), ()))
    (lh, ll), (rh, rl) = left, right
    dot = functools.partial(
        lax.dot_general, dimension_numbers=dims, preferred_element_type=jnp.float32
    )
    return dot(lh, rh) + (dot(lh, rl) + dot(ll, rh))


def positions():
    pole = lax.axis_index("pole")
    blk = lax.axis_index("blk")
    return pole // (NH * NC), (pole // NC) % NH, pole % NC, blk // NZ, blk % NZ, blk


def column_kernel(sizes, lists, slots, weights, *refs):
    width, listed, nodes, share = sizes
    pieces = refs[: NY * NZ]
    inverse, diag, send, keep, whole, tiles, left_h, left_l, mixed, total, sems = refs[NY * NZ :]
    my_x, my_h, my_c, my_y, my_z, blk = positions()
    wr = weights[0, 0]
    wi = weights[0, 1]

    def slot_of(k, m):
        return slots[lists[k, m]]

    def copy(k, m):
        row = pl.multiple_of(slot_of(k, m) * width, width)
        at = k * listed + m
        return pltpu.make_async_copy(
            inverse.at[0, pl.ds(row, width), :], tiles.at[at], sems.at[at]
        )

    found = []
    for k in range(nodes):
        place = jnp.int32(-1)
        for m in range(listed):
            place = jnp.where(slot_of(k, m) == blk, m, place)
        found.append(place)

        @pl.when(place >= 0)
        def _(k=k):
            for m in range(listed):
                copy(k, m).start()

    for dy in range(NY):
        for dz in range(NZ):
            owner = ((my_y + dy) % NY) * NZ + (my_z + dz) % NZ
            piece = pieces[dy * NZ + dz]
            for k in range(nodes):
                row = pl.multiple_of(owner * share, 8)
                whole[k, pl.ds(row, share), :] = piece[k * share : (k + 1) * share, :]

    strip = width // (NX * NH * NC)

    def deal(k, t, value_ref):
        at = pl.multiple_of((k * (listed + 1) + t) * strip, strip)
        for rx in range(NX):
            for rh in range(NH):
                for rc, out in ((0, keep), (1, send)):
                    row = (((my_x + rx) % NX) * NH + (my_h + rh) % NH) * NC + (my_c + rc) % NC
                    row = pl.multiple_of(row * strip, strip)
                    out[rx, rh, pl.ds(at, strip), :] = value_ref[pl.ds(row, strip), :]

    own = jnp.where(blk == 0, 1.0, 0.0).astype(jnp.float32)
    for k in range(nodes):
        place = found[k]
        total[...] = jnp.zeros_like(total)

        @pl.when(place < 0)
        def _(k=k):
            at = k * (listed + 1) * strip
            zeros = jnp.zeros((NX, NH, listed * strip, width), jnp.float32)
            keep[:, :, at : at + listed * strip, :] = zeros
            send[:, :, at : at + listed * strip, :] = zeros

        @pl.when(place >= 0)
        def _(k=k, place=place):
            row = pl.multiple_of(place * width, width)
            tile = whole[k, pl.ds(row, width), :]
            real = tile[:, :width]
            imag = tile[:, width:]
            w_real = (wr * real - wi * imag).T
            w_imag = (wr * imag + wi * real).T
            for r, c, value in (
                (0, 0, w_imag),
                (0, 1, w_real),
                (1, 0, w_real),
                (1, 1, -w_imag),
            ):
                high, low = split(value)
                left_h[r * width : (r + 1) * width, c * width : (c + 1) * width] = high
                left_l[r * width : (r + 1) * width, c * width : (c + 1) * width] = low

            @pl.loop(0, listed)
            def _(m):
                copy(k, m).wait()
                right = split(tiles[k * listed + m])
                product = dot3((left_h[...], left_l[...]), right, ((1,), (1,)))
                upper = product[:width]
                lower = product[width:]
                mixed[...] = -upper
                deal(k, m, mixed)
                row = pl.multiple_of(m * width, width)
                factor = whole[k, pl.ds(row, width), :]
                total[...] += dot3(split(upper), split(factor[:, :width]), ((1,), (0,)))
                total[...] += dot3(split(lower), split(factor[:, width:]), ((1,), (0,)))

        base = own * (wr * diag[0, k, :, width:] + wi * diag[0, k, :, :width])
        mixed[...] = base + total[...].T
        deal(k, listed, mixed)


def place_kernel(sizes, lists, slots, values, send, keep):
    width, listed, nodes, strip = sizes
    _, _, _, my_y, my_z, _ = positions()
    for rz in range(NZ):
        for ry, out in ((0, keep), (1, send)):
            dest = ((my_y + ry) % NY) * NZ + (my_z + rz) % NZ
            for k in range(nodes):
                found = jnp.int32(-1)
                for m in range(listed):
                    found = jnp.where(slots[lists[k, m]] == dest, m, found)
                row = (k * (listed + 1) + jnp.maximum(found, 0)) * strip
                row = pl.multiple_of(row, strip)
                value = values[pl.ds(row, strip), :]
                out[rz, k] = jnp.where(found >= 0, value, jnp.zeros_like(value))
            for k in range(nodes):
                row = (k * (listed + 1) + listed) * strip
                if rz == 0:
                    out[NZ, k] = values[row : row + strip, :]


def local(inverse, factor, diag_inverse, residues, row_lists, block_slot):
    width = diag_inverse.shape[2]
    nodes, listed = row_lists.shape
    share = factor.shape[2]
    strip = width // (NX * NH * NC)
    f32 = jnp.float32
    vmem = pl.BlockSpec(memory_space=pltpu.VMEM)
    smem = pl.BlockSpec(memory_space=pltpu.SMEM)
    hbm = pl.BlockSpec(memory_space=pl.ANY)

    mine = factor.reshape(nodes * share, 2 * width)
    other = lax.ppermute(mine, "blk", FLIP_Y)
    pieces = [[None] * NZ for _ in range(NY)]
    pieces[0][0], pieces[1][0] = mine, other
    up = [mine, other]
    down = [mine, other]
    for step in range(1, NZ // 2):
        up = [lax.ppermute(v, "blk", shift_z(1)) for v in up]
        down = [lax.ppermute(v, "blk", shift_z(-1)) for v in down]
        for dy in range(NY):
            pieces[dy][-step] = up[dy]
            pieces[dy][step] = down[dy]
    pieces[0][NZ // 2] = lax.ppermute(up[0], "blk", shift_z(1))
    pieces[1][NZ // 2] = lax.ppermute(down[1], "blk", shift_z(-1))
    flat = [p for row in pieces for p in row]

    rows = nodes * (listed + 1) * strip
    half = jax.ShapeDtypeStruct((NX, NH, rows, width), f32)
    send, keep = pl.pallas_call(
        functools.partial(column_kernel, (width, listed, nodes, share)),
        out_shape=(half, half),
        in_specs=[smem] * 3 + [vmem] * (NY * NZ) + [hbm, vmem],
        out_specs=(vmem, vmem),
        scratch_shapes=[
            pltpu.VMEM((nodes, listed * width, 2 * width), f32),
            pltpu.VMEM((nodes * listed, width, 2 * width), f32),
            pltpu.VMEM((2 * width, 2 * width), jnp.bfloat16),
            pltpu.VMEM((2 * width, 2 * width), jnp.bfloat16),
            pltpu.VMEM((width, width), f32),
            pltpu.VMEM((width, width), f32),
            pltpu.SemaphoreType.DMA((nodes * listed,)),
        ],
        name="column",
    )(row_lists, block_slot, residues, *flat, inverse, diag_inverse)

    arrived = lax.ppermute(send, "pole", FLIP_C)
    parts = [keep[rx] + arrived[rx] for rx in range(NX)]
    summed = parts[0]
    for rx in range(1, NX):
        summed = summed + lax.ppermute(parts[rx], "pole", shift_x(rx))
    values = summed[0] + lax.ppermute(summed[1], "pole", FLIP_H)

    spread = jax.ShapeDtypeStruct((NZ + 1, nodes, strip, width), f32)
    send, keep = pl.pallas_call(
        functools.partial(place_kernel, (width, listed, nodes, strip)),
        out_shape=(spread, spread),
        in_specs=[smem, smem, vmem],
        out_specs=(vmem, vmem),
        name="place",
    )(row_lists, block_slot, values)
    both = keep + lax.ppermute(send, "blk", FLIP_Y)
    density_rows = both[0]
    density_diag = both[NZ]
    for rz in range(1, NZ):
        message = jnp.stack([both[rz], both[NZ]])
        arrived = lax.ppermute(message, "blk", shift_z(rz))
        density_rows = density_rows + arrived[0]
        density_diag = density_diag + arrived[1]
    return density_rows, density_diag


def solution(mesh):
    in_specs = (
        P("pole", None, "blk"),
        P("pole", None, "blk", None),
        P("pole", None, None, None),
        P("pole", None),
        P(),
        P(),
    )
    out_specs = (P(None, "pole", "blk"), P(None, "pole", None))
    return jax.shard_map(local, mesh=mesh, in_specs=in_specs, out_specs=out_specs, check_vma=False)
```
